128 devices in a mesh: leaf: 16 (over x, z), row: 8 (over y, core).
Axes of the slice: x: 4, y: 4, z: 4, core: 2. Of those that a mesh axis runs over, the one named last changes fastest.
Arguments:
- right_side: float32 [16, 2048, 1024], P('leaf', 'row'), may hold values from -6 to 6
- lower_rows: float32 [16, 2048, 2048], P('leaf', 'row'), may hold values from -0.125 to 0.125
- diag_inverse: float32 [16, 2048, 256], P('leaf', 'row'), may hold values from -0.375 to 0.375
- update_rows: float32 [16, 4096, 2048], P('leaf', 'row'), may hold values from -0.125 to 0.125
- owner_map: int32 [16, 32], P('leaf', 'row'), may hold values from 0 to 127, as said below
- block_counts: int32 [16], P('leaf'), may hold values from 1 to 32, as said below
- ancestor_rhs: float32 [16, 8192, 1024], P('leaf', 'row'), may hold values from -6 to 6
- ancestor_inverse: float32 [16, 8192, 128], P('leaf', 'row'), may hold values from -0.5 to 0.5
Outputs:
- solution: float32 [16, 2048, 1024], P('leaf', 'row')
- parent_front_solution_rows: float32 [16, 8192, 1024], P('leaf', 'row')
The draws below stay inside these ranges and needn't reach their ends.
Inputs may be any that keep to these rules, and one draw needn't show every extreme that they name: `owner_map`: among the 4 blocks b with the same b // 4 of one front, the values g // 8 are distinct. `block_counts`: some front has all its blocks live.
All inputs are finite; a program needn't handle non-finite values.
Results may differ from the reference program's by a relative error of at most 0.0001.
Values sent between devices are 32-bit elements; how exact they have to be, the bound alone decides.
A program may use at most 320 MiB of HBM per device.

```python
import jax
import jax.numpy as jnp
from jax import lax

PIV = 2048
UPD = 4096
BLK = 128
RHS = 1024
TB = 8
FRONTS = 16
PANEL = 256
N_ROW = 8


def draw_owner_map(key, part):
    nblocks = UPD // N_ROW // BLK
    keys = jax.random.split(key, 2)
    total = FRONTS * N_ROW
    owner_keys = jax.random.split(keys[0], total)
    owners = jax.vmap(lambda k: jax.random.permutation(k, FRONTS)[:nblocks])(owner_keys)
    slots = jax.random.randint(keys[1], (total, nblocks), 0, TB)
    return (owners * TB + slots).reshape(FRONTS, N_ROW * nblocks).astype(jnp.int32)


def draw_block_counts(key, part):
    whole = UPD // BLK
    keys = jax.random.split(key, 2)
    counts = jax.random.randint(keys[0], (FRONTS,), 1, whole + 1)
    pick = jax.random.randint(keys[1], (), 0, FRONTS)
    return jnp.where(jnp.arange(FRONTS) == pick, whole, counts).astype(jnp.int32)


def levels(stream_key, dims, pieces, least, high):
    factor_of, own = 1.0, jax.random.fold_in(stream_key, 6)
    for dim, parts in pieces:
        steps = jnp.exp(jax.random.uniform(jax.random.fold_in(own, dim), (parts,), jnp.float32, least / len(pieces), high / len(pieces)))
        factor_of = factor_of * jnp.repeat(steps, dims[dim] // parts).reshape([-1 if axis == dim else 1 for axis in range(len(dims))])
    return factor_of


def noise(own_key, extent, spread, most, cuts=(), kind=jnp.bfloat16):
    values = spread * jax.random.normal(own_key, extent, jnp.float32)
    if cuts:
        values = values * levels(own_key, extent, cuts, -0.22, 0.18)
    return jnp.clip(values, -most, most).astype(kind)


def setup_inputs(seed: int = 0) -> dict:
    streams_of = jax.random.split(jax.random.key(seed), 9)
    right_side = noise(streams_of[0], (FRONTS, PIV, RHS), 1.0, 6.0, ((0, 16), (1, 8)), jnp.float32)
    lower_rows = noise(streams_of[1], (FRONTS, PIV, PIV), PIV ** -0.5, 0.125, ((0, 16), (1, 8)), jnp.float32)
    diag_inverse = noise(streams_of[2], (FRONTS, PIV, PANEL), PANEL ** -0.5, 0.375, ((0, 16), (1, 8)), jnp.float32)
    update_rows = noise(streams_of[3], (FRONTS, UPD, PIV), PIV ** -0.5, 0.125, ((0, 16), (1, 8)), jnp.float32)
    owner_map = draw_owner_map(jax.random.fold_in(streams_of[8], 71), 0)
    block_counts = draw_block_counts(jax.random.fold_in(streams_of[8], 71), 0)
    ancestor_rhs = noise(streams_of[6], (FRONTS, N_ROW * TB * BLK, RHS), 1.0, 6.0, ((0, 16), (1, 8)), jnp.float32)
    ancestor_inverse = noise(streams_of[7], (FRONTS, N_ROW * TB * BLK, BLK), BLK ** -0.5, 0.5, ((0, 16), (1, 8)), jnp.float32)
    return {"right_side": right_side, "lower_rows": lower_rows, "diag_inverse": diag_inverse, "update_rows": update_rows, "owner_map": owner_map, "block_counts": block_counts, "ancestor_rhs": ancestor_rhs, "ancestor_inverse": ancestor_inverse}


def reference(right_side, lower_rows, diag_inverse, update_rows, owner_map, block_counts, ancestor_rhs, ancestor_inverse):
    topmost_front = lax.Precision.HIGHEST
    panel = PIV // N_ROW
    nblocks = UPD // N_ROW // BLK
    solved = []
    for k in range(N_ROW):
        accum = jnp.zeros((FRONTS, panel, RHS), jnp.float32)
        for j in range(k):
            block = lower_rows[:, k * panel:(k + 1) * panel, j * panel:(j + 1) * panel]
            accum = accum + jnp.einsum("fpq,fqc->fpc", block, solved[j], precision=topmost_front)
        inverse = diag_inverse[:, k * panel:(k + 1) * panel, :]
        solved.append(jnp.einsum("fpq,fqc->fpc", inverse, right_side[:, k * panel:(k + 1) * panel] - accum, precision=topmost_front))
    solution = jnp.concatenate(solved, axis=1)
    update = jnp.einsum("fuq,fqc->fuc", update_rows, solution, precision=topmost_front)
    blocks = update.reshape(FRONTS, N_ROW, nblocks, BLK, RHS)
    index = jnp.arange(N_ROW * nblocks, dtype=jnp.int32).reshape(N_ROW, nblocks)
    live = (index[None] < block_counts[:, None, None]).astype(jnp.float32)
    targets = owner_map.reshape(FRONTS, N_ROW, nblocks)
    onehot = (targets[..., None] == jnp.arange(FRONTS * TB, dtype=jnp.int32)).astype(jnp.float32) * live[..., None]
    summed = jnp.einsum("frjg,frjbc->rgbc", onehot, blocks, precision=topmost_front)
    summed = summed.reshape(N_ROW, FRONTS, TB, BLK, RHS).transpose(1, 0, 2, 3, 4).reshape(FRONTS, N_ROW * TB, BLK, RHS)
    remaining_right_side = ancestor_rhs.reshape(FRONTS, N_ROW * TB, BLK, RHS) - summed
    inverse = ancestor_inverse.reshape(FRONTS, N_ROW * TB, BLK, BLK)
    parent_front_solution_rows = jnp.einsum("fnab,fnbc->fnac", inverse, remaining_right_side, precision=topmost_front)
    return solution, parent_front_solution_rows.reshape(FRONTS, N_ROW * TB * BLK, RHS)
```

```python
import jax
import jax.numpy as jnp
from jax import lax
from jax.experimental import pallas as pl
from jax.experimental.pallas import tpu as pltpu
from jax.sharding import PartitionSpec as P

BLK = 128
CW = 128
F32 = jnp.float32
BF16 = jnp.bfloat16
MESH = pl.DeviceIdType.MESH


def split(value):
    high = value.astype(BF16)
    return high, (value - high.astype(F32)).astype(BF16)


def product(left_high, left_low, right):
    right_high, right_low = split(right)
    n = right.shape[1]
    both = jnp.dot(
        left_high, jnp.concatenate([right_high, right_low], axis=1), preferred_element_type=F32
    )
    cross = jnp.dot(left_low, right_high, preferred_element_type=F32)
    return both[:, :n] + (both[:, n:] + cross)


def kernel(
    meta_ref, rhs_hbm, low_hbm, dinv_hbm, upd_hbm, ancr_hbm, anci_hbm,
    sol_out, anc_out,
    rhs_v, low_v, dinv_v, raw_v, ancr_v, anci_v,
    dh, dl, wh, wl, uh, ul, ah, al,
    acc_v, sol_v, upd_v, held, part, total, near_p, near_m, far_p, far_m, metas, table,
    rhs_sem, low_sem, dinv_sem, upd_sem, ancr_sem, anci_sem, meta_sem, sol_sem, anc_sem,
    panel_recv, own_send, fwd_send, relay_send,
    z1_send, z1_recv, x_send, x_recv, z2_send, z2_recv, mz_send, mz_recv, mx_send, mx_recv,
):
    chunks = sol_v.shape[0]
    leaf, row = lax.axis_index("leaf"), lax.axis_index("row")
    x, z = leaf // 4, lax.rem(leaf, 4)
    y, core = row // 2, lax.rem(row, 2)
    xp, xo, xm = (lax.rem(x + i, 4) for i in (1, 2, 3))
    zp, zo, zm = (lax.rem(z + i, 4) for i in (1, 2, 3))
    yp, ym = lax.rem(y + 1, 4), lax.rem(y + 3, 4)

    def device(xx, zz, rr):
        return {"leaf": xx * 4 + zz, "row": rr}

    sibling = device(x, z, y * 2 + 1 - core)
    to_yp, to_ym = device(x, z, yp * 2 + 1 - core), device(x, z, ym * 2 + 1 - core)
    to_zp, to_zo, to_zm = (device(x, i, row) for i in (zp, zo, zm))
    to_xp, to_xo, to_xm = (device(i, z, row) for i in (xp, xo, xm))

    def remote(src, dst, send, recv, to):
        return pltpu.make_async_remote_copy(
            src_ref=src, dst_ref=dst, send_sem=send, recv_sem=recv, device_id=to, device_id_type=MESH
        )

    def lanes(c):
        return pl.ds(pl.multiple_of(c * CW, CW), CW)

    load_dinv = pltpu.make_async_copy(dinv_hbm, dinv_v, dinv_sem)
    load_upd = pltpu.make_async_copy(upd_hbm, raw_v, upd_sem)
    load_anci = pltpu.make_async_copy(anci_hbm, anci_v, anci_sem)

    def load_rhs(c):
        return pltpu.make_async_copy(rhs_hbm.at[:, lanes(c)], rhs_v.at[c], rhs_sem.at[c])

    def load_ancr(c):
        return pltpu.make_async_copy(ancr_hbm.at[:, lanes(c)], ancr_v.at[c], ancr_sem.at[c])

    def load_low(k):
        columns = pl.ds(pl.multiple_of(k * 256, 256), 256)
        return pltpu.make_async_copy(low_hbm.at[:, columns], low_v.at[k], low_sem.at[k])

    def store_sol(c):
        return pltpu.make_async_copy(sol_v.at[c, row], sol_out.at[:, lanes(c)], sol_sem.at[c])

    def store_anc(c):
        return pltpu.make_async_copy(ancr_v.at[c], anc_out.at[:, lanes(c)], anc_sem.at[c])

    def own_copy(c, i):
        place = sol_v.at[c, row]
        return remote(
            place, place, own_send.at[i, c], panel_recv.at[row, c], (sibling, to_yp, to_ym)[i]
        )

    def forward(c, k, i):
        place = sol_v.at[c, k]
        return remote(place, place, fwd_send.at[i, c], panel_recv.at[k, c], sibling)

    def relay(c, k):
        place = sol_v.at[c, k]
        return remote(place, place, relay_send.at[c], panel_recv.at[k, c], to_yp)

    def arrive(c, k):
        owner_core = lax.rem(k, 2)
        away = lax.rem(y - k // 2 + 4, 4)
        forward(c, k, 0).wait_recv()
        crossed = owner_core == 1 - core
        straight = owner_core == core

        @pl.when((away == 1) & crossed)
        def _():
            relay(c, k).start()
            forward(c, k, 0).start()

        @pl.when((away == 2) & straight)
        def _():
            forward(c, k, 1).start()

        @pl.when((away == 3) & crossed)
        def _():
            forward(c, k, 2).start()

    def z1(c, i):
        if i == 0:
            src, dst, to = upd_v.at[c, pl.ds(128 * zp, 128)], held.at[c, pl.ds(512 * x + 128 * z, 128)], to_zp
        elif i == 1:
            src, dst, to = upd_v.at[c, pl.ds(128 * zm, 128)], held.at[c, pl.ds(512 * x + 128 * z, 128)], to_zm
        elif i == 2:
            src, dst, to = upd_v.at[c, pl.ds(128 * zo, 64)], near_p.at[c], to_zp
        elif i == 3:
            src, dst, to = upd_v.at[c, pl.ds(128 * zo + 64, 64)], near_m.at[c], to_zm
        elif i == 4:
            src, dst, to = near_p.at[c], held.at[c, pl.ds(512 * x + 128 * zm, 64)], to_zp
        else:
            src, dst, to = near_m.at[c], held.at[c, pl.ds(512 * x + 128 * zp + 64, 64)], to_zm
        return remote(src, dst, z1_send.at[i, c], z1_recv.at[i, c], to)

    def xc(c, i):
        if i == 0:
            place, to = held.at[c, pl.ds(512 * x, 512)], to_xp
        elif i == 1:
            place, to = held.at[c, pl.ds(512 * x, 512)], to_xm
        elif i == 2:
            place, to = held.at[c, pl.ds(512 * xm, 256)], to_xp
        else:
            place, to = held.at[c, pl.ds(512 * xp + 256, 256)], to_xm
        return remote(place, place, x_send.at[i, c], x_recv.at[i, c], to)

    def z2(c, i):
        if i == 0:
            src, dst, to = part.at[c, pl.ds(256 * zp, 256)], total.at[c, pl.ds(256 * z, 256)], to_zp
        elif i == 1:
            src, dst, to = part.at[c, pl.ds(256 * zm, 256)], total.at[c, pl.ds(256 * z, 256)], to_zm
        elif i == 2:
            src, dst, to = part.at[c, pl.ds(256 * zo, 128)], far_p.at[c], to_zp
        elif i == 3:
            src, dst, to = part.at[c, pl.ds(256 * zo + 128, 128)], far_m.at[c], to_zm
        elif i == 4:
            src, dst, to = far_p.at[c], total.at[c, pl.ds(256 * zm, 128)], to_zp
        else:
            src, dst, to = far_m.at[c], total.at[c, pl.ds(256 * zp + 128, 128)], to_zm
        return remote(src, dst, z2_send.at[i, c], z2_recv.at[i, c], to)

    def mz(i):
        return remote(
            meta_ref, metas.at[x, z], mz_send.at[i], mz_recv.at[i], (to_zp, to_zo, to_zm)[i]
        )

    def mx(i):
        return remote(
            metas.at[x], metas.at[x], mx_send.at[i], mx_recv.at[i], (to_xp, to_xo, to_xm)[i]
        )

    own_meta = pltpu.make_async_copy(meta_ref, metas.at[x, z], meta_sem)

    load_dinv.start()
    load_rhs(0).start()

    @pl.loop(0, row)
    def _(k):
        load_low(k).start()

    @pl.loop(1, chunks)
    def _(c):
        load_rhs(c).start()

    load_upd.start()
    load_anci.start()

    @pl.loop(0, chunks)
    def _(c):
        load_ancr(c).start()

    barrier = pltpu.get_barrier_semaphore()
    partners = (sibling, to_yp, to_ym, to_zp, to_zo, to_zm, to_xp, to_xo, to_xm)
    for to in partners:
        pl.semaphore_signal(barrier, inc=1, device_id=to, device_id_type=MESH)
    pl.semaphore_wait(barrier, len(partners))

    own_meta.start()
    for i in range(3):
        mz(i).start()

    load_dinv.wait()
    high, low = split(dinv_v[...])
    dh[...] = high
    dl[...] = low

    @pl.loop(0, row)
    def _(k):
        load_low(k).wait()
        high, low = split(product(dh[...], dl[...], low_v[k]))
        wh[k] = high
        wl[k] = low

    def split_update_rows():
        load_upd.wait()

        @pl.loop(0, 16)
        def _(q):
            source = pl.multiple_of(lax.rem(q, 4) * 128 + (q // 4) * 32, 32)
            target = pl.multiple_of(q * 32, 32)
            high, low = split(raw_v[pl.ds(source, 32), :])
            uh[pl.ds(target, 32), :] = high
            ul[pl.ds(target, 32), :] = low

    pl.when(y > 0)(split_update_rows)

    def solve(c):
        load_rhs(c).wait()
        acc_v[...] = product(dh[...], dl[...], rhs_v[c])

        @pl.loop(0, row)
        def _(k):
            arrive(c, k)
            acc_v[...] -= product(wh[k], wl[k], sol_v[c, k])

        sol_v[c, row] = acc_v[...]
        for i in range(3):
            own_copy(c, i).start()
        store_sol(c).start()

    def update(c):
        @pl.loop(row + 1, 8)
        def _(k):
            arrive(c, k)

        upd_v[c] = product(uh[...], ul[...], sol_v[c].reshape(2048, CW))
        held[c, pl.ds(pl.multiple_of(512 * x + 128 * z, 128), 128), :] = upd_v[
            c, pl.ds(pl.multiple_of(128 * z, 128), 128), :
        ]
        for i in (2, 3, 0, 1):
            z1(c, i).start()

    def meta_over_z():
        own_meta.wait()
        for i in range(3):
            mz(i).wait_recv()
        for i in range(3):
            mx(i).start()

    def make_table():
        for i in range(3):
            mx(i).wait_recv()
        meta = jnp.sum(metas[...].reshape(16, 8, 128), axis=0)
        wanted = (lax.broadcasted_iota(jnp.int32, (32, 128), 0) + (32 * x + 1)).astype(F32)
        row0 = jnp.broadcast_to(meta[0:1, :], (32, 128))
        table[...] = jnp.where(row0 == wanted, 1.0, 0.0).astype(BF16)
        anci = anci_v[...]
        high, low = split(anci)
        ah[...] = high
        al[...] = low

    def reduce(c):
        @pl.loop(0, 8)
        def _(g):
            for i in range(4):
                r = g * 4 + i
                pieces = held[c, pl.ds(r, 64, stride=32), :]
                high, low = split(pieces)
                part[c, pl.ds(r, 32, stride=32), :] = jnp.dot(
                    table[...], jnp.concatenate([high, low], axis=0), preferred_element_type=F32
                )

        own = pl.ds(pl.multiple_of(256 * z, 256), 256)
        total[c, own, :] = part[c, own, :]
        for i in (2, 3, 0, 1):
            z2(c, i).start()

    def ancestors(c):
        load_ancr(c).wait()
        for slot in range(8):
            rows = pl.ds(slot * 128, 128)
            summed = jnp.concatenate(
                [total[c, pl.ds(i * 256 + slot * 32, 32), :] for i in range(4)], axis=0
            )
            ancr_v[c, rows, :] = product(ah[rows, :], al[rows, :], ancr_v[c, rows, :] - summed)
        store_anc(c).start()

    ahead = 3 - y

    @pl.loop(0, chunks + 3 + ahead)
    def _(t):
        c0 = t - ahead
        c1, c2, c3 = c0 - 1, c0 - 2, c0 - 3

        def valid(c):
            return (c >= 0) & (c < chunks)

        @pl.when(valid(c1))
        def _():
            z1(c1, 2).wait_recv()
            z1(c1, 4).start()
            z1(c1, 3).wait_recv()
            z1(c1, 5).start()

        @pl.when(valid(c2))
        def _():
            xc(c2, 0).wait_recv()
            xc(c2, 2).start()
            xc(c2, 1).wait_recv()
            xc(c2, 3).start()

        @pl.when(valid(c3))
        def _():
            z2(c3, 2).wait_recv()
            z2(c3, 4).start()
            z2(c3, 3).wait_recv()
            z2(c3, 5).start()

        @pl.when(t < chunks)
        def _():
            solve(t)

        @pl.when(t == 0)
        def _():
            meta_over_z()
            pl.when(y == 0)(split_update_rows)

        @pl.when(valid(c0))
        def _():
            update(c0)

        @pl.when(valid(c1))
        def _():
            for i in (0, 1, 4, 5):
                z1(c1, i).wait_recv()
            xc(c1, 0).start()
            xc(c1, 1).start()

        @pl.when(c2 == 0)
        def _():
            load_anci.wait()
            make_table()

        @pl.when(valid(c2))
        def _():
            xc(c2, 2).wait_recv()
            xc(c2, 3).wait_recv()
            reduce(c2)

        @pl.when(valid(c3))
        def _():
            for i in (0, 1, 4, 5):
                z2(c3, i).wait_recv()
            ancestors(c3)

    for i in range(3):
        mz(i).wait_send()
        mx(i).wait_send()

    @pl.loop(0, chunks)
    def _(c):
        for i in range(3):
            own_copy(c, i).wait_send()
            forward(c, 0, i).wait_send()
        relay(c, 0).wait_send()
        for i in range(6):
            z1(c, i).wait_send()
            z2(c, i).wait_send()
        for i in range(4):
            xc(c, i).wait_send()
        store_sol(c).wait()
        store_anc(c).wait()


def body(
    right_side,
    lower_rows,
    diag_inverse,
    update_rows,
    owner_map,
    block_counts,
    ancestor_rhs,
    ancestor_inverse,
):
    leaf, row = lax.axis_index("leaf"), lax.axis_index("row")
    nblocks = owner_map.shape[1]
    columns = right_side.shape[2]
    chunks = columns // CW
    lane = lax.rem(jnp.arange(128, dtype=jnp.int32), 64)
    block = lax.rem(lane, nblocks)
    live = (lane // nblocks == leaf) & (row * nblocks + block < block_counts[0])
    owners = jnp.zeros((128,), jnp.int32)
    for j in range(nblocks):
        owners = jnp.where(block == j, owner_map[0, j], owners)
    meta = jnp.where(live, owners + 1, 0).astype(F32)
    meta = jnp.broadcast_to(meta[None], (8, 128))

    dma = pltpu.SemaphoreType.DMA
    vmem = pltpu.VMEM
    scratch = [
        vmem((chunks, 256, CW), F32),
        vmem((8, 256, 256), F32),
        vmem((256, 256), F32),
        vmem((512, 2048), F32),
        vmem((chunks, 1024, CW), F32),
        vmem((1024, 128), F32),
        vmem((256, 256), BF16),
        vmem((256, 256), BF16),
        vmem((8, 256, 256), BF16),
        vmem((8, 256, 256), BF16),
        vmem((512, 2048), BF16),
        vmem((512, 2048), BF16),
        vmem((1024, 128), BF16),
        vmem((1024, 128), BF16),
        vmem((256, CW), F32),
        vmem((chunks, 8, 256, CW), F32),
        vmem((chunks, 512, CW), F32),
        vmem((chunks, 2048, CW), F32),
        vmem((chunks, 1024, CW), F32),
        vmem((chunks, 1024, CW), F32),
        vmem((chunks, 64, CW), F32),
        vmem((chunks, 64, CW), F32),
        vmem((chunks, 128, CW), F32),
        vmem((chunks, 128, CW), F32),
        vmem((4, 4, 8, 128), F32),
        vmem((32, 128), BF16),
        dma((chunks,)),
        dma((8,)),
        dma,
        dma,
        dma((chunks,)),
        dma,
        dma,
        dma((chunks,)),
        dma((chunks,)),
        dma((8, chunks)),
        dma((3, chunks)),
        dma((3, chunks)),
        dma((chunks,)),
        dma((6, chunks)),
        dma((6, chunks)),
        dma((4, chunks)),
        dma((4, chunks)),
        dma((6, chunks)),
        dma((6, chunks)),
        dma((3,)),
        dma((3,)),
        dma((3,)),
        dma((3,)),
    ]
    anywhere = pl.BlockSpec(memory_space=pl.ANY)
    sol, anc = pl.pallas_call(
        kernel,
        out_shape=(
            jax.ShapeDtypeStruct((256, columns), F32),
            jax.ShapeDtypeStruct((1024, columns), F32),
        ),
        in_specs=[pl.BlockSpec(memory_space=pltpu.VMEM)] + [anywhere] * 6,
        out_specs=(anywhere, anywhere),
        scratch_shapes=scratch,
        compiler_params=pltpu.CompilerParams(
            collective_id=0, has_side_effects=True, vmem_limit_bytes=67043328
        ),
    )(
        meta,
        right_side[0],
        lower_rows[0],
        diag_inverse[0],
        update_rows[0],
        ancestor_rhs[0],
        ancestor_inverse[0],
    )
    return sol[None], anc[None]


def solution(mesh):
    in_specs = (
        P("leaf", "row", None),
        P("leaf", "row", None),
        P("leaf", "row", None),
        P("leaf", "row", None),
        P("leaf", "row"),
        P("leaf"),
        P("leaf", "row", None),
        P("leaf", "row", None),
    )
    out_specs = (P("leaf", "row", None), P("leaf", "row", None))
    return jax.shard_map(body, mesh=mesh, in_specs=in_specs, out_specs=out_specs, check_vma=False)
```

```python
import jax
import jax.numpy as jnp
from jax import lax
from jax.experimental import pallas as pl
from jax.experimental.pallas import tpu as pltpu
from jax.sharding import PartitionSpec as P

BLK = 128
CW = 128
AHEAD = (8, 5, 3, 1)
LAST_Y = 3
STAGES = (0, 1, 2, 3)
F32 = jnp.float32
BF16 = jnp.bfloat16
MESH = pl.DeviceIdType.MESH


def split(value):
    high = value.astype(BF16)
    return high, (value - high.astype(F32)).astype(BF16)


def product(left_high, left_low, right):
    right_high, right_low = split(right)
    n = right.shape[1]
    both = jnp.dot(
        left_high, jnp.concatenate([right_high, right_low], axis=1), preferred_element_type=F32
    )
    cross = jnp.dot(left_low, right_high, preferred_element_type=F32)
    return both[:, :n] + (both[:, n:] + cross)


def kernel(
    owner_ref, count_ref, rhs_hbm, low_hbm, dinv_hbm, upd_hbm, ancr_hbm, anci_hbm,
    sol_out, anc_out,
    rhs_v, low_v, dinv_v, raw_v, ancr_v, anci_v,
    dh, dl, wh, wl, uh, ul, ah, al,
    acc_v, sol_v, upd_v, held, part, total, meta_ref, metas, table,
    rhs_sem, low_sem, dinv_sem, upd_sem, ancr_sem, anci_sem, meta_sem, sol_sem, anc_sem,
    panel_recv, own_send, fwd_send,
    cut_send, cut_recv, ring_send, ring_recv, sum_send, sum_recv, mz_send, mz_recv, mx_send, mx_recv,
):
    chunks = sol_v.shape[0]
    leaf, row = lax.axis_index("leaf"), lax.axis_index("row")
    x, z = leaf // 4, lax.rem(leaf, 4)
    y, core = row // 2, lax.rem(row, 2)
    yp, ym = lax.rem(y + 1, 4), lax.rem(y + 3, 4)

    def device(xx, zz, rr):
        return {"leaf": xx * 4 + zz, "row": rr}

    sibling = device(x, z, y * 2 + 1 - core)
    to_yp, to_ym = device(x, z, yp * 2 + 1 - core), device(x, z, ym * 2 + 1 - core)
    to_yo = device(x, z, lax.rem(y + 2, 4) * 2 + core)
    to_z = [device(x, lax.rem(z + i, 4), row) for i in (1, 2, 3)]
    to_x = [device(lax.rem(x + i, 4), z, row) for i in (1, 2, 3)]
    cut_at, cut_to = (z, x), (to_z, to_x)
    ring_at, ring_to = (x, z), (to_x, to_z)

    def remote(src, dst, send, recv, to):
        return pltpu.make_async_remote_copy(
            src_ref=src, dst_ref=dst, send_sem=send, recv_sem=recv, device_id=to, device_id_type=MESH
        )

    def lanes(c):
        return pl.ds(pl.multiple_of(c * CW, CW), CW)

    def rows(start, size):
        return pl.ds(pl.multiple_of(start, size), size)

    load_dinv = pltpu.make_async_copy(dinv_hbm, dinv_v, dinv_sem)
    load_upd = pltpu.make_async_copy(upd_hbm, raw_v, upd_sem)
    load_anci = pltpu.make_async_copy(anci_hbm, anci_v, anci_sem)

    def load_rhs(c):
        return pltpu.make_async_copy(rhs_hbm.at[:, lanes(c)], rhs_v.at[c], rhs_sem.at[c])

    def load_ancr(c):
        return pltpu.make_async_copy(ancr_hbm.at[:, lanes(c)], ancr_v.at[c], ancr_sem.at[c])

    def load_low(k):
        columns = pl.ds(pl.multiple_of(k * 256, 256), 256)
        return pltpu.make_async_copy(low_hbm.at[:, columns], low_v.at[k], low_sem.at[k])

    def store_sol(c):
        return pltpu.make_async_copy(sol_v.at[c, row], sol_out.at[:, lanes(c)], sol_sem.at[c])

    def store_anc(c):
        return pltpu.make_async_copy(ancr_v.at[c], anc_out.at[:, lanes(c)], anc_sem.at[c])

    def own_copy(c, i):
        place = sol_v.at[c, row]
        return remote(
            place, place, own_send.at[i, c], panel_recv.at[row, c], (sibling, to_yp, to_ym, to_yo)[i]
        )

    def forward(c, k, i):
        place = sol_v.at[c, k]
        return remote(place, place, fwd_send.at[i, c], panel_recv.at[k, c], sibling)

    def route(k):
        away = lax.rem(y - k // 2 + 4, 4)
        same = lax.rem(k, 2) == core
        return away, ((away == 2) & same) | ((lax.rem(away, 2) == 1) & jnp.logical_not(same))

    def take(c, k):
        away, direct = route(k)

        @pl.when(direct)
        def _():
            forward(c, k, 0).wait_recv()
            forward(c, k, away - 1).start()

    def need(c, k):
        _, direct = route(k)

        @pl.when(jnp.logical_not(direct))
        def _():
            forward(c, k, 0).wait_recv()

    def cut(o, c, i):
        there = lax.rem(cut_at[o] + 1 + i, 4)
        return remote(
            upd_v.at[c, rows(256 * o + 64 * there, 64)],
            held.at[c, rows(1024 * o + 256 * ring_at[o] + 64 * cut_at[o], 64)],
            cut_send.at[o, i, c], cut_recv.at[o, i, c], cut_to[o][i],
        )

    def ring(o, c, i):
        origin = lax.rem(ring_at[o] + (0, 0, 0, 0, 3, 1)[i], 4)
        half = (0, 1, 1, 0, 0, 1)[i]
        place = held.at[c, rows(1024 * o + 256 * origin + 128 * half, 128)]
        to = ring_to[o][(0, 0, 2, 2, 0, 2)[i]]
        return remote(place, place, ring_send.at[o, i, c], ring_recv.at[o, i, c], to)

    def summed(o, c, i):
        there = lax.rem(cut_at[o] + 1 + i, 4)
        return remote(
            part.at[c, rows(512 * o + 128 * there, 128)],
            total.at[c, rows(512 * o + 128 * cut_at[o], 128)],
            sum_send.at[o, i, c], sum_recv.at[o, i, c], cut_to[o][i],
        )

    def mz(i):
        return remote(meta_ref, metas.at[x, z], mz_send.at[i], mz_recv.at[i], to_z[i])

    def mx(i):
        return remote(metas.at[x], metas.at[x], mx_send.at[i], mx_recv.at[i], to_x[i])

    own_meta = pltpu.make_async_copy(meta_ref, metas.at[x, z], meta_sem)

    load_dinv.start()
    load_rhs(0).start()

    lane = lax.broadcasted_iota(jnp.int32, (8, 128), 1) & 63
    order = lax.broadcasted_iota(jnp.int32, (8, 128), 0)
    block, source = lane & 3, lane >> 2
    place = jnp.where(order == 0, source, ((source & 3) << 2) | (source >> 2))
    owner = jnp.zeros((8, 128), jnp.int32)
    for j in range(4):
        owner = jnp.where(block == j, owner_ref[j] + 1, owner)
    live = (place == leaf) & (order < 2) & (block + row * 4 < count_ref[0])
    meta_ref[...] = jnp.where(live, owner, 0).astype(F32)

    @pl.loop(0, row)
    def _(k):
        load_low(k).start()

    @pl.loop(1, chunks)
    def _(c):
        load_rhs(c).start()

    load_upd.start()
    load_anci.start()

    @pl.loop(0, chunks)
    def _(c):
        load_ancr(c).start()

    barrier = pltpu.get_barrier_semaphore()
    partners = [sibling, to_yp, to_ym, to_yo, *to_z, *to_x]
    for to in partners:
        pl.semaphore_signal(barrier, inc=1, device_id=to, device_id_type=MESH)
    pl.semaphore_wait(barrier, len(partners))

    own_meta.start()
    for i in range(3):
        mz(i).start()

    load_dinv.wait()
    high, low = split(dinv_v[...])
    dh[...] = high
    dl[...] = low

    @pl.loop(0, row)
    def _(k):
        load_low(k).wait()
        high, low = split(product(dh[...], dl[...], low_v[k]))
        columns = pl.ds(pl.multiple_of(lax.rem(k, 2) * 256, 256), 256)
        wh[k // 2, :, columns] = high
        wl[k // 2, :, columns] = low

    early = y <= 1

    def start_rhs(c):
        load_rhs(c).wait()
        rhs_v[c] = product(dh[...], dl[...], rhs_v[c])

    def split_update_rows():
        load_upd.wait()

        @pl.loop(0, 32)
        def _(q):
            source = lax.rem(q, 4) * 128 + (q // 16) * 64 + lax.rem(q // 4, 4) * 16
            high, low = split(raw_v[rows(source, 16), :])
            uh[rows(q * 16, 16), :] = high
            ul[rows(q * 16, 16), :] = low

    @pl.when(jnp.logical_not(early))
    def _():
        @pl.loop(0, chunks)
        def _(c):
            start_rhs(c)

        split_update_rows()

    def take_early(c):
        @pl.loop(0, row)
        def _(k):
            take(c, k)

    def take_late(c, start, stop):
        @pl.loop(jnp.maximum(row + 1, start), stop)
        def _(k):
            take(c, k)

    def solve(c):
        @pl.when(early)
        def _():
            start_rhs(c)

        acc_v[...] = rhs_v[c]

        @pl.loop(0, y)
        def _(j):
            @pl.when(c == 0)
            def _():
                take(c, 2 * j)
                take(c, 2 * j + 1)

            need(c, 2 * j)
            need(c, 2 * j + 1)
            acc_v[...] -= product(
                wh[j], wl[j], sol_v[c, pl.ds(2 * j, 2)].reshape(512, CW)
            )

        @pl.when(core == 1)
        def _():
            need(c, 2 * y)
            acc_v[...] -= product(wh[y, :, pl.ds(0, 256)], wl[y, :, pl.ds(0, 256)], sol_v[c, 2 * y])

        sol_v[c, row] = acc_v[...]
        for i in range(4):
            own_copy(c, i).start()
        store_sol(c).start()

    def update(c):
        @pl.loop(row + 1, 6)
        def _(k):
            need(c, k)

        first, last = pl.ds(0, 1536), pl.ds(1536, 512)
        upd_v[c] = product(uh[:, first], ul[:, first], sol_v[c, pl.ds(0, 6)].reshape(1536, CW))

        @pl.when(c == 0)
        def _():
            take_late(c, 6, 8)

        @pl.loop(jnp.maximum(row + 1, 6), 8)
        def _(k):
            need(c, k)

        upd_v[c] += product(uh[:, last], ul[:, last], sol_v[c, pl.ds(6, 2)].reshape(512, CW))
        for o in range(2):
            own = rows(1024 * o + 256 * ring_at[o] + 64 * cut_at[o], 64)
            held[c, own, :] = upd_v[c, rows(256 * o + 64 * cut_at[o], 64), :]
        for i in (1, 0, 2):
            for o in range(2):
                cut(o, c, i).start()

    def meta_over_z():
        own_meta.wait()
        for i in range(3):
            mz(i).wait_recv()
        for i in range(3):
            mx(i).start()

    def make_tables():
        load_anci.wait()
        high, low = split(anci_v[...])
        ah[...] = high
        al[...] = low
        for i in range(3):
            mx(i).wait_recv()
        meta = jnp.sum(metas[...].reshape(16, 8, 128), axis=0)
        target = lax.broadcasted_iota(jnp.int32, (32, 128), 0)
        wanted = (32 * x + target, target // 8 * 32 + 8 * z + lax.rem(target, 8))
        for o in range(2):
            sources = jnp.broadcast_to(meta[o : o + 1, :], (32, 128))
            table[o] = jnp.where(sources == (wanted[o] + 1).astype(F32), 1.0, 0.0).astype(BF16)

    def start_ring(c):
        for o in range(2):
            for i in range(3):
                cut(o, c, i).wait_recv()
            for i in (0, 2, 1, 3):
                ring(o, c, i).start()

    def pass_on(c):
        for o in range(2):
            for i in (0, 2):
                ring(o, c, i).wait_recv()
                ring(o, c, 4 + i // 2).start()

    def reduce(c):
        for o in range(2):
            for i in (1, 3, 4, 5):
                ring(o, c, i).wait_recv()

        @pl.loop(0, 2)
        def _(g):
            for i in range(8):
                for o in range(2):
                    r = g * 8 + i
                    pieces = held[c, pl.ds(1024 * o + r, 64, stride=16), :]
                    high, low = split(pieces)
                    part[c, pl.ds(512 * o + r, 32, stride=16), :] = jnp.dot(
                        table[o], jnp.concatenate([high, low], axis=0), preferred_element_type=F32
                    )

        for o in range(2):
            own = rows(512 * o + 128 * cut_at[o], 128)
            total[c, own, :] = part[c, own, :]
        for i in (1, 0, 2):
            for o in range(2):
                summed(o, c, i).start()

    def ancestors(c):
        for o in range(2):
            for i in range(3):
                summed(o, c, i).wait_recv()
        load_ancr(c).wait()
        for slot in range(8):
            here = pl.ds(slot * 128, 128)
            gone = jnp.concatenate(
                [total[c, pl.ds(i * 128 + slot * 16, 16), :] for i in range(8)], axis=0
            )
            ancr_v[c, here, :] = product(ah[here, :], al[here, :], ancr_v[c, here, :] - gone)
        store_anc(c).start()

    ahead = jnp.where(y == 0, AHEAD[0], jnp.where(y == 1, AHEAD[1], jnp.where(y == 2, AHEAD[2], AHEAD[3])))

    @pl.loop(0, chunks + ahead + STAGES[-1])
    def _(t):
        c0 = t - ahead

        def stage(k, work):
            c = c0 - STAGES[k]
            pl.when((c >= 0) & (c < chunks))(lambda: work(c))

        @pl.when(c0 == 0)
        def _():
            meta_over_z()
            pl.when(early)(split_update_rows)

        @pl.when((t > 0) & (t < chunks) & (y < LAST_Y))
        def _():
            take_early(t)

        @pl.when((c0 >= 0) & (c0 < chunks))
        def _():
            update(c0)

        @pl.when((t > 0) & (t < chunks) & (y >= LAST_Y))
        def _():
            take_early(t)

        @pl.when(t < chunks)
        def _():
            solve(t)

        stage(1, pass_on)

        @pl.when((c0 + 1 >= 0) & (c0 + 1 < chunks))
        def _():
            take_late(c0 + 1, 0, jnp.where(c0 + 1 == 0, 6, 8))

        @pl.when(c0 == 1)
        def _():
            make_tables()

        stage(2, reduce)
        stage(3, ancestors)
        stage(0, start_ring)

    for i in range(3):
        mz(i).wait_send()
        mx(i).wait_send()

    @pl.loop(0, chunks)
    def _(c):
        for i in range(4):
            own_copy(c, i).wait_send()
        for i in range(3):
            forward(c, 0, i).wait_send()
        for o in range(2):
            for i in range(3):
                cut(o, c, i).wait_send()
                summed(o, c, i).wait_send()
            for i in range(6):
                ring(o, c, i).wait_send()
        store_sol(c).wait()
        store_anc(c).wait()


def copy_kernel(sol_in, anc_in, sol_out, anc_out, buffer, load_sem, store_sem):
    loads, stores = [], []
    for i in range(10):
        source, target, j = (sol_in, sol_out, i) if i < 2 else (anc_in, anc_out, i - 2)
        here = pl.ds(j * 128, 128)
        loads.append(pltpu.make_async_copy(source.at[here], buffer.at[i], load_sem.at[i]))
        stores.append(pltpu.make_async_copy(buffer.at[i], target.at[here], store_sem.at[i]))
    for load in loads:
        load.start()
    for load, store in zip(loads, stores):
        load.wait()
        store.start()
    for store in stores:
        store.wait()


def body(
    right_side,
    lower_rows,
    diag_inverse,
    update_rows,
    owner_map,
    block_counts,
    ancestor_rhs,
    ancestor_inverse,
):
    columns = right_side.shape[2]
    chunks = columns // CW
    dma = pltpu.SemaphoreType.DMA
    vmem = pltpu.VMEM
    scratch = [
        vmem((chunks, 256, CW), F32),
        vmem((8, 256, 256), F32),
        vmem((256, 256), F32),
        vmem((512, 2048), F32),
        vmem((chunks, 1024, CW), F32),
        vmem((1024, 128), F32),
        vmem((256, 256), BF16),
        vmem((256, 256), BF16),
        vmem((4, 256, 512), BF16),
        vmem((4, 256, 512), BF16),
        vmem((512, 2048), BF16),
        vmem((512, 2048), BF16),
        vmem((1024, 128), BF16),
        vmem((1024, 128), BF16),
        vmem((256, CW), F32),
        vmem((chunks, 8, 256, CW), F32),
        vmem((chunks, 512, CW), F32),
        vmem((chunks, 2048, CW), F32),
        vmem((chunks, 1024, CW), F32),
        vmem((chunks, 1024, CW), F32),
        vmem((8, 128), F32),
        vmem((4, 4, 8, 128), F32),
        vmem((2, 32, 128), BF16),
        dma((chunks,)),
        dma((8,)),
        dma,
        dma,
        dma((chunks,)),
        dma,
        dma,
        dma((chunks,)),
        dma((chunks,)),
        dma((8, chunks)),
        dma((4, chunks)),
        dma((3, chunks)),
        dma((2, 3, chunks)),
        dma((2, 3, chunks)),
        dma((2, 6, chunks)),
        dma((2, 6, chunks)),
        dma((2, 3, chunks)),
        dma((2, 3, chunks)),
        dma((3,)),
        dma((3,)),
        dma((3,)),
        dma((3,)),
    ]
    anywhere = pl.BlockSpec(memory_space=pl.ANY)
    sol, anc = pl.pallas_call(
        kernel,
        out_shape=(
            jax.ShapeDtypeStruct((256, columns), F32),
            jax.ShapeDtypeStruct((1024, columns), F32),
        ),
        in_specs=[pl.BlockSpec(memory_space=pltpu.SMEM)] * 2 + [anywhere] * 6,
        out_specs=(anywhere, anywhere),
        scratch_shapes=scratch,
        compiler_params=pltpu.CompilerParams(
            collective_id=0, has_side_effects=True, vmem_limit_bytes=67043328
        ),
    )(
        owner_map[0],
        block_counts,
        right_side[0],
        lower_rows[0],
        diag_inverse[0],
        update_rows[0],
        ancestor_rhs[0],
        ancestor_inverse[0],
    )
    sol, anc = pl.pallas_call(
        copy_kernel,
        out_shape=(
            jax.ShapeDtypeStruct((256, columns), F32),
            jax.ShapeDtypeStruct((1024, columns), F32),
        ),
        in_specs=[anywhere] * 2,
        out_specs=(anywhere, anywhere),
        scratch_shapes=[vmem((10, 128, columns), F32), dma((10,)), dma((10,))],
        compiler_params=pltpu.CompilerParams(vmem_limit_bytes=67043328),
    )(sol, anc)
    return sol[None], anc[None]


def solution(mesh):
    in_specs = (
        P("leaf", "row", None),
        P("leaf", "row", None),
        P("leaf", "row", None),
        P("leaf", "row", None),
        P("leaf", "row"),
        P("leaf"),
        P("leaf", "row", None),
        P("leaf", "row", None),
    )
    out_specs = (P("leaf", "row", None), P("leaf", "row", None))
    return jax.shard_map(body, mesh=mesh, in_specs=in_specs, out_specs=out_specs, check_vma=False)
```

```python
import jax
import jax.numpy as jnp
from jax import lax
from jax.experimental import pallas as pl
from jax.experimental.pallas import tpu as pltpu
from jax.sharding import PartitionSpec as P

BLK = 128
CW = 128
AHEAD = (8, 5, 3, 1)
LAST_Y = 1
STAGES = (0, 1, 2, 3)
F32 = jnp.float32
BF16 = jnp.bfloat16
MESH = pl.DeviceIdType.MESH


def split(value):
    high = value.astype(BF16)
    return high, (value - high.astype(F32)).astype(BF16)


def product(left_high, left_low, right):
    right_high, right_low = split(right)
    n = right.shape[1]
    both = jnp.dot(
        left_high, jnp.concatenate([right_high, right_low], axis=1), preferred_element_type=F32
    )
    cross = jnp.dot(left_low, right_high, preferred_element_type=F32)
    return both[:, :n] + (both[:, n:] + cross)


def kernel(
    owner_ref, count_ref, rhs_hbm, low_hbm, dinv_hbm, upd_hbm, ancr_hbm, anci_hbm,
    sol_out, anc_out,
    rhs_v, low_v, dinv_v, raw_v, ancr_v, anci_v,
    dh, dl, wh, wl, uh, ul, ah, al,
    acc_v, sol_v, upd_v, held, part, total, meta_ref, metas, table,
    rhs_sem, low_sem, dinv_sem, upd_sem, ancr_sem, anci_sem, meta_sem, sol_sem, anc_sem,
    panel_recv, own_send, fwd_send,
    cut_send, cut_recv, ring_send, ring_recv, sum_send, sum_recv, mz_send, mz_recv, mx_send, mx_recv,
):
    chunks = sol_v.shape[0]
    leaf, row = lax.axis_index("leaf"), lax.axis_index("row")
    x, z = leaf // 4, lax.rem(leaf, 4)
    y, core = row // 2, lax.rem(row, 2)
    yp, ym = lax.rem(y + 1, 4), lax.rem(y + 3, 4)

    def device(xx, zz, rr):
        return {"leaf": xx * 4 + zz, "row": rr}

    sibling = device(x, z, y * 2 + 1 - core)
    to_yp, to_ym = device(x, z, yp * 2 + 1 - core), device(x, z, ym * 2 + 1 - core)
    to_yo = device(x, z, lax.rem(y + 2, 4) * 2 + core)
    to_z = [device(x, lax.rem(z + i, 4), row) for i in (1, 2, 3)]
    to_x = [device(lax.rem(x + i, 4), z, row) for i in (1, 2, 3)]
    cut_at, cut_to = (z, x), (to_z, to_x)
    ring_at, ring_to = (x, z), (to_x, to_z)

    def remote(src, dst, send, recv, to):
        return pltpu.make_async_remote_copy(
            src_ref=src, dst_ref=dst, send_sem=send, recv_sem=recv, device_id=to, device_id_type=MESH
        )

    def lanes(c):
        return pl.ds(pl.multiple_of(c * CW, CW), CW)

    def rows(start, size):
        return pl.ds(pl.multiple_of(start, size), size)

    load_dinv = pltpu.make_async_copy(dinv_hbm, dinv_v, dinv_sem)
    load_upd = pltpu.make_async_copy(upd_hbm, raw_v, upd_sem)
    load_anci = pltpu.make_async_copy(anci_hbm, anci_v, anci_sem)

    def load_rhs(c):
        return pltpu.make_async_copy(rhs_hbm.at[:, lanes(c)], rhs_v.at[c], rhs_sem.at[c])

    def load_ancr(c):
        return pltpu.make_async_copy(ancr_hbm.at[:, lanes(c)], ancr_v.at[c], ancr_sem.at[c])

    def load_low(k):
        columns = pl.ds(pl.multiple_of(k * 256, 256), 256)
        return pltpu.make_async_copy(low_hbm.at[:, columns], low_v.at[k], low_sem.at[k])

    def store_sol(c):
        return pltpu.make_async_copy(sol_v.at[c, row], sol_out.at[:, lanes(c)], sol_sem.at[c])

    def store_anc(c):
        return pltpu.make_async_copy(ancr_v.at[c], anc_out.at[:, lanes(c)], anc_sem.at[c])

    def own_copy(c, i):
        place = sol_v.at[c, row]
        return remote(
            place, place, own_send.at[i, c], panel_recv.at[row, c], (sibling, to_yp, to_ym, to_yo)[i]
        )

    def forward(c, k, i):
        place = sol_v.at[c, k]
        return remote(place, place, fwd_send.at[i, c], panel_recv.at[k, c], sibling)

    def route(k):
        away = lax.rem(y - k // 2 + 4, 4)
        same = lax.rem(k, 2) == core
        return away, ((away == 2) & same) | ((lax.rem(away, 2) == 1) & jnp.logical_not(same))

    def take(c, k):
        away, direct = route(k)

        @pl.when(direct)
        def _():
            forward(c, k, 0).wait_recv()
            forward(c, k, away - 1).start()

    def need(c, k):
        _, direct = route(k)

        @pl.when(jnp.logical_not(direct))
        def _():
            forward(c, k, 0).wait_recv()

    def cut(o, c, i):
        there = lax.rem(cut_at[o] + 1 + i, 4)
        return remote(
            upd_v.at[c, rows(256 * o + 64 * there, 64)],
            held.at[c, rows(1024 * o + 256 * ring_at[o] + 64 * cut_at[o], 64)],
            cut_send.at[o, i, c], cut_recv.at[o, i, c], cut_to[o][i],
        )

    def ring(o, c, i):
        origin = lax.rem(ring_at[o] + (0, 0, 0, 0, 3, 1)[i], 4)
        half = (0, 1, 1, 0, 0, 1)[i]
        place = held.at[c, rows(1024 * o + 256 * origin + 128 * half, 128)]
        to = ring_to[o][(0, 0, 2, 2, 0, 2)[i]]
        return remote(place, place, ring_send.at[o, i, c], ring_recv.at[o, i, c], to)

    def summed(o, c, i):
        there = lax.rem(cut_at[o] + 1 + i, 4)
        return remote(
            part.at[c, rows(512 * o + 128 * there, 128)],
            total.at[c, rows(512 * o + 128 * cut_at[o], 128)],
            sum_send.at[o, i, c], sum_recv.at[o, i, c], cut_to[o][i],
        )

    def mz(i):
        return remote(meta_ref, metas.at[x, z], mz_send.at[i], mz_recv.at[i], to_z[i])

    def mx(i):
        return remote(metas.at[x], metas.at[x], mx_send.at[i], mx_recv.at[i], to_x[i])

    own_meta = pltpu.make_async_copy(meta_ref, metas.at[x, z], meta_sem)

    load_dinv.start()
    load_rhs(0).start()

    lane = lax.broadcasted_iota(jnp.int32, (8, 128), 1) & 63
    order = lax.broadcasted_iota(jnp.int32, (8, 128), 0)
    block, source = lane & 3, lane >> 2
    place = jnp.where(order == 0, source, ((source & 3) << 2) | (source >> 2))
    owner = jnp.zeros((8, 128), jnp.int32)
    for j in range(4):
        owner = jnp.where(block == j, owner_ref[j] + 1, owner)
    live = (place == leaf) & (order < 2) & (block + row * 4 < count_ref[0])
    meta_ref[...] = jnp.where(live, owner, 0).astype(F32)

    @pl.loop(0, row)
    def _(k):
        load_low(k).start()

    @pl.loop(1, chunks)
    def _(c):
        load_rhs(c).start()

    load_upd.start()
    load_anci.start()

    @pl.loop(0, chunks)
    def _(c):
        load_ancr(c).start()

    barrier = pltpu.get_barrier_semaphore()
    partners = [sibling, to_yp, to_ym, to_yo, *to_z, *to_x]
    for to in partners:
        pl.semaphore_signal(barrier, inc=1, device_id=to, device_id_type=MESH)
    pl.semaphore_wait(barrier, len(partners))

    own_meta.start()
    for i in range(3):
        mz(i).start()

    load_dinv.wait()
    high, low = split(dinv_v[...])
    dh[...] = high
    dl[...] = low

    @pl.loop(0, row)
    def _(k):
        load_low(k).wait()
        high, low = split(product(dh[...], dl[...], low_v[k]))
        columns = pl.ds(pl.multiple_of(lax.rem(k, 2) * 256, 256), 256)
        wh[k // 2, :, columns] = high
        wl[k // 2, :, columns] = low

    early = y <= 1

    def start_rhs(c):
        load_rhs(c).wait()
        rhs_v[c] = product(dh[...], dl[...], rhs_v[c])

    def split_update_rows():
        load_upd.wait()

        @pl.loop(0, 32)
        def _(q):
            source = lax.rem(q, 4) * 128 + (q // 16) * 64 + lax.rem(q // 4, 4) * 16
            high, low = split(raw_v[rows(source, 16), :])
            uh[rows(q * 16, 16), :] = high
            ul[rows(q * 16, 16), :] = low

    @pl.when(jnp.logical_not(early))
    def _():
        @pl.loop(0, chunks)
        def _(c):
            start_rhs(c)

        split_update_rows()

    def take_early(c):
        @pl.loop(0, row)
        def _(k):
            take(c, k)

    def take_late(c, start, stop):
        @pl.loop(jnp.maximum(row + 1, start), stop)
        def _(k):
            take(c, k)

    def solve(c):
        @pl.when(early)
        def _():
            start_rhs(c)

        acc_v[...] = rhs_v[c]

        @pl.loop(0, y)
        def _(j):
            @pl.when(c == 0)
            def _():
                take(c, 2 * j)
                take(c, 2 * j + 1)

            need(c, 2 * j)
            need(c, 2 * j + 1)
            acc_v[...] -= product(
                wh[j], wl[j], sol_v[c, pl.ds(2 * j, 2)].reshape(512, CW)
            )

        @pl.when(core == 1)
        def _():
            need(c, 2 * y)
            acc_v[...] -= product(wh[y, :, pl.ds(0, 256)], wl[y, :, pl.ds(0, 256)], sol_v[c, 2 * y])

        sol_v[c, row] = acc_v[...]
        own_copy(c, 0).start()

        @pl.when(y == 3)
        def _():
            own_copy(c, 3).start()

        own_copy(c, 1).start()
        own_copy(c, 2).start()

        @pl.when(y < 3)
        def _():
            own_copy(c, 3).start()

        store_sol(c).start()

    def update(c):
        @pl.loop(row + 1, 6)
        def _(k):
            need(c, k)

        first, last = pl.ds(0, 1536), pl.ds(1536, 512)
        upd_v[c] = product(uh[:, first], ul[:, first], sol_v[c, pl.ds(0, 6)].reshape(1536, CW))

        @pl.when(c == 0)
        def _():
            take_late(c, 6, 8)

        @pl.loop(jnp.maximum(row + 1, 6), 8)
        def _(k):
            need(c, k)

        upd_v[c] += product(uh[:, last], ul[:, last], sol_v[c, pl.ds(6, 2)].reshape(512, CW))
        for o in range(2):
            own = rows(1024 * o + 256 * ring_at[o] + 64 * cut_at[o], 64)
            held[c, own, :] = upd_v[c, rows(256 * o + 64 * cut_at[o], 64), :]
        for i in (1, 0, 2):
            for o in range(2):
                cut(o, c, i).start()

    def meta_over_z():
        own_meta.wait()
        for i in range(3):
            mz(i).wait_recv()
        for i in range(3):
            mx(i).start()

    def make_tables():
        load_anci.wait()
        high, low = split(anci_v[...])
        ah[...] = high
        al[...] = low
        for i in range(3):
            mx(i).wait_recv()
        meta = jnp.sum(metas[...].reshape(16, 8, 128), axis=0)
        target = lax.broadcasted_iota(jnp.int32, (32, 128), 0)
        wanted = (32 * x + target, target // 8 * 32 + 8 * z + lax.rem(target, 8))
        for o in range(2):
            sources = jnp.broadcast_to(meta[o : o + 1, :], (32, 128))
            table[o] = jnp.where(sources == (wanted[o] + 1).astype(F32), 1.0, 0.0).astype(BF16)

    def start_ring(c):
        for o in range(2):
            for i in range(3):
                cut(o, c, i).wait_recv()
            for i in (0, 2, 1, 3):
                ring(o, c, i).start()

    def pass_on(c):
        for o in range(2):
            for i in (0, 2):
                ring(o, c, i).wait_recv()
                ring(o, c, 4 + i // 2).start()

    def reduce(c):
        for o in range(2):
            for i in (1, 3, 4, 5):
                ring(o, c, i).wait_recv()

        @pl.loop(0, 2)
        def _(g):
            for i in range(8):
                for o in range(2):
                    r = g * 8 + i
                    pieces = held[c, pl.ds(1024 * o + r, 64, stride=16), :]
                    high, low = split(pieces)
                    part[c, pl.ds(512 * o + r, 32, stride=16), :] = jnp.dot(
                        table[o], jnp.concatenate([high, low], axis=0), preferred_element_type=F32
                    )

        for o in range(2):
            own = rows(512 * o + 128 * cut_at[o], 128)
            total[c, own, :] = part[c, own, :]
        for i in (1, 0, 2):
            for o in range(2):
                summed(o, c, i).start()

    def ancestors(c):
        for o in range(2):
            for i in range(3):
                summed(o, c, i).wait_recv()
        load_ancr(c).wait()
        for slot in range(8):
            here = pl.ds(slot * 128, 128)
            gone = jnp.concatenate(
                [total[c, pl.ds(i * 128 + slot * 16, 16), :] for i in range(8)], axis=0
            )
            ancr_v[c, here, :] = product(ah[here, :], al[here, :], ancr_v[c, here, :] - gone)
        store_anc(c).start()

    ahead = jnp.where(y == 0, AHEAD[0], jnp.where(y == 1, AHEAD[1], jnp.where(y == 2, AHEAD[2], AHEAD[3])))

    @pl.loop(0, chunks + ahead + STAGES[-1])
    def _(t):
        c0 = t - ahead

        def stage(k, work):
            c = c0 - STAGES[k]
            pl.when((c >= 0) & (c < chunks))(lambda: work(c))

        @pl.when(c0 == 0)
        def _():
            meta_over_z()
            pl.when(early)(split_update_rows)

        @pl.when((t > 0) & (t < chunks) & (y < LAST_Y))
        def _():
            take_early(t)

        @pl.when((c0 >= 0) & (c0 < chunks))
        def _():
            update(c0)

        @pl.when((t > 0) & (t < chunks) & (y >= LAST_Y))
        def _():
            take_early(t)

        @pl.when(t < chunks)
        def _():
            solve(t)

        stage(1, pass_on)

        @pl.when((c0 + 1 >= 0) & (c0 + 1 < chunks))
        def _():
            take_late(c0 + 1, 0, jnp.where(c0 + 1 == 0, 6, 8))

        @pl.when(c0 == 1)
        def _():
            make_tables()

        stage(2, reduce)
        stage(0, start_ring)
        stage(3, ancestors)

    for i in range(3):
        mz(i).wait_send()
        mx(i).wait_send()

    @pl.loop(0, chunks)
    def _(c):
        for i in range(4):
            own_copy(c, i).wait_send()
        for i in range(3):
            forward(c, 0, i).wait_send()
        for o in range(2):
            for i in range(3):
                cut(o, c, i).wait_send()
                summed(o, c, i).wait_send()
            for i in range(6):
                ring(o, c, i).wait_send()
        store_sol(c).wait()
        store_anc(c).wait()


def copy_kernel(sol_in, anc_in, sol_out, anc_out, buffer, load_sem, store_sem):
    loads, stores = [], []
    for i in range(10):
        source, target, j = (sol_in, sol_out, i) if i < 2 else (anc_in, anc_out, i - 2)
        here = pl.ds(j * 128, 128)
        loads.append(pltpu.make_async_copy(source.at[here], buffer.at[i], load_sem.at[i]))
        stores.append(pltpu.make_async_copy(buffer.at[i], target.at[here], store_sem.at[i]))
    for load in loads:
        load.start()
    for load, store in zip(loads, stores):
        load.wait()
        store.start()
    for store in stores:
        store.wait()


def body(
    right_side,
    lower_rows,
    diag_inverse,
    update_rows,
    owner_map,
    block_counts,
    ancestor_rhs,
    ancestor_inverse,
):
    columns = right_side.shape[2]
    chunks = columns // CW
    dma = pltpu.SemaphoreType.DMA
    vmem = pltpu.VMEM
    scratch = [
        vmem((chunks, 256, CW), F32),
        vmem((8, 256, 256), F32),
        vmem((256, 256), F32),
        vmem((512, 2048), F32),
        vmem((chunks, 1024, CW), F32),
        vmem((1024, 128), F32),
        vmem((256, 256), BF16),
        vmem((256, 256), BF16),
        vmem((4, 256, 512), BF16),
        vmem((4, 256, 512), BF16),
        vmem((512, 2048), BF16),
        vmem((512, 2048), BF16),
        vmem((1024, 128), BF16),
        vmem((1024, 128), BF16),
        vmem((256, CW), F32),
        vmem((chunks, 8, 256, CW), F32),
        vmem((chunks, 512, CW), F32),
        vmem((chunks, 2048, CW), F32),
        vmem((chunks, 1024, CW), F32),
        vmem((chunks, 1024, CW), F32),
        vmem((8, 128), F32),
        vmem((4, 4, 8, 128), F32),
        vmem((2, 32, 128), BF16),
        dma((chunks,)),
        dma((8,)),
        dma,
        dma,
        dma((chunks,)),
        dma,
        dma,
        dma((chunks,)),
        dma((chunks,)),
        dma((8, chunks)),
        dma((4, chunks)),
        dma((3, chunks)),
        dma((2, 3, chunks)),
        dma((2, 3, chunks)),
        dma((2, 6, chunks)),
        dma((2, 6, chunks)),
        dma((2, 3, chunks)),
        dma((2, 3, chunks)),
        dma((3,)),
        dma((3,)),
        dma((3,)),
        dma((3,)),
    ]
    anywhere = pl.BlockSpec(memory_space=pl.ANY)
    sol, anc = pl.pallas_call(
        kernel,
        out_shape=(
            jax.ShapeDtypeStruct((256, columns), F32),
            jax.ShapeDtypeStruct((1024, columns), F32),
        ),
        in_specs=[pl.BlockSpec(memory_space=pltpu.SMEM)] * 2 + [anywhere] * 6,
        out_specs=(anywhere, anywhere),
        scratch_shapes=scratch,
        compiler_params=pltpu.CompilerParams(
            collective_id=0, has_side_effects=True, vmem_limit_bytes=67043328
        ),
    )(
        owner_map[0],
        block_counts,
        right_side[0],
        lower_rows[0],
        diag_inverse[0],
        update_rows[0],
        ancestor_rhs[0],
        ancestor_inverse[0],
    )
    sol, anc = pl.pallas_call(
        copy_kernel,
        out_shape=(
            jax.ShapeDtypeStruct((256, columns), F32),
            jax.ShapeDtypeStruct((1024, columns), F32),
        ),
        in_specs=[anywhere] * 2,
        out_specs=(anywhere, anywhere),
        scratch_shapes=[vmem((10, 128, columns), F32), dma((10,)), dma((10,))],
        compiler_params=pltpu.CompilerParams(vmem_limit_bytes=67043328),
    )(sol, anc)
    return sol[None], anc[None]


def solution(mesh):
    in_specs = (
        P("leaf", "row", None),
        P("leaf", "row", None),
        P("leaf", "row", None),
        P("leaf", "row", None),
        P("leaf", "row"),
        P("leaf"),
        P("leaf", "row", None),
        P("leaf", "row", None),
    )
    out_specs = (P("leaf", "row", None), P("leaf", "row", None))
    return jax.shard_map(body, mesh=mesh, in_specs=in_specs, out_specs=out_specs, check_vma=False)
```
